256 devices in a mesh: rows: 4 (over z_hi, core), cols: 64 (over y, z_lo, x).
Axes of the slice: x: 4, y: 4, z: 8 (z_hi: 2, z_lo: 4; z = z_hi * 4 + z_lo), core: 2. Of those that a mesh axis runs over, the one named last changes fastest.
Arguments:
- weight: float32 [26624, 16384], P('rows', 'cols'), may hold values from -6 to 6
- sign_bits: int32 [16384], P('cols'), may hold values from 0 to 1
Outputs:
- rotated: bfloat16 [26624, 16384], P(('rows', 'cols'))
- column_peak: float32 [16384], P('cols')
The draws below stay inside these ranges and needn't reach their ends.
Inputs may be any that keep to these rules, and one draw needn't show every extreme that they name: Input column m is flipped in sign where sign_bits[m] is 0.
All inputs are finite; a program needn't handle non-finite values.
Results may differ from the reference program's by a relative error of at most 0.001.
Values sent between devices are 32-bit elements; how exact they have to be, the bound alone decides.
A program may use at most 64 MiB of HBM per device.

```python
import jax
import jax.numpy as jnp
from jax import lax

K = 16384
ROWS = 26624
N_COLS = 64


def set_ends(drawn, rng, smallest, high):
    shape = drawn.shape
    spot = [jax.random.randint(jax.random.fold_in(rng, axis), (), 0, shape[axis]) for axis in range(len(shape))]
    drawn = drawn.at[tuple(spot)].set(smallest)
    longest = shape.index(max(shape))
    spot[longest] = (spot[longest] + 1) % shape[longest]
    return drawn.at[tuple(spot)].set(high)


def levels(own_key, shape, shards, low, largest):
    level, own = 1.0, jax.random.fold_in(own_key, 6)
    for dim, shards_of in shards:
        draws = jnp.exp(jax.random.uniform(jax.random.fold_in(own, dim), (shards_of,), jnp.float32, low / len(shards), largest / len(shards)))
        level = level * jnp.repeat(draws, shape[dim] // shards_of).reshape([-1 if axis == dim else 1 for axis in range(len(shape))])
    return level


def centred(stream_key, dims, scale, limit, cuts=(), kind=jnp.bfloat16):
    gain = levels(stream_key, dims, cuts, -0.22, 0.18) if cuts else 1.0
    entries = jax.random.normal(stream_key, dims, jnp.float32) * scale * gain
    return jnp.minimum(jnp.maximum(entries, -limit), limit).astype(kind)


def setup_inputs(seed: int = 0) -> dict:
    splits = jax.random.split(jax.random.key(seed), 3)
    weight = centred(splits[0], (ROWS, K), 1.0, 6.0, ((0, 4), (1, 64)), jnp.float32)
    sign_bits = set_ends(jax.random.randint(splits[1], (K,), 0, 2), jax.random.fold_in(splits[1], 1), 0, 1).astype(jnp.int32)
    return {"weight": weight, "sign_bits": sign_bits}


def sylvester(order):
    index = jnp.arange(order, dtype=jnp.int32)
    common = jnp.bitwise_and(index[:, None], index[None, :])
    parity = jnp.zeros((order, order), jnp.int32)
    for place in range(max(order.bit_length() - 1, 1)):
        parity = jnp.bitwise_xor(parity, jnp.bitwise_and(jnp.right_shift(common, place), 1))
    return (1 - 2 * parity).astype(jnp.float32)


def reference(weight, sign_bits):
    local = K // N_COLS
    sign = (2 * sign_bits - 1).astype(jnp.float32)
    flipped = weight * sign[None, :]
    blocks = flipped.reshape(ROWS, N_COLS, local)
    inner = jnp.einsum("adj,jk->adk", blocks, sylvester(local), precision=lax.Precision.HIGHEST)
    outer = jnp.einsum("adk,de->aek", inner, sylvester(N_COLS), precision=lax.Precision.HIGHEST)
    exact = outer.reshape(ROWS, K) * jnp.float32(1.0 / (K ** 0.5))
    column_peak = jnp.max(jnp.abs(exact), axis=0)
    return exact.astype(jnp.bfloat16), column_peak
```

```python
import functools

import jax
import jax.numpy as jnp
from jax import lax
from jax.experimental import pallas as pl
from jax.experimental.pallas import tpu as pltpu
from jax.sharding import PartitionSpec as P

MESH = pl.DeviceIdType.MESH
BLOCK = 16
TILE = 256


def sylvester(order, scale):
    row = lax.broadcasted_iota(jnp.int32, (order, order), 0)
    column = lax.broadcasted_iota(jnp.int32, (order, order), 1)
    parity = row & column
    shift = order.bit_length() // 2
    while shift:
        parity = parity ^ (parity >> shift)
        shift //= 2
    return ((1 - 2 * (parity & 1)).astype(jnp.float32) * scale).astype(jnp.bfloat16)


def butterfly(values):
    values, step = list(values), 1
    while step < len(values):
        for start in range(0, len(values), 2 * step):
            for k in range(start, start + step):
                a, b = values[k], values[k + step]
                values[k], values[k + step] = a + b, a - b
        step *= 2
    return values


def kernel(
    n, n_rows, chunks, scale,
    w_ref, bits_ref, out_ref, peak_ref,
    recv, signs, work, table, staged, peaks, row_peaks, col_in, own, row_in,
    send_sem, recv_sem, local_sem, out_sem, peak_sem,
):
    me = lax.axis_index("cols")
    my_row = lax.axis_index("rows")
    total, local = recv.shape[1], recv.shape[2]

    def peer_of(s):
        z, x, y = s & 3, (s >> 2) & 3, s >> 4
        return me ^ (y * 16 + z * 4 + x)

    mine = pltpu.make_async_copy(
        w_ref.at[pl.ds(pl.multiple_of(me * total, 8), total)], recv.at[me], local_sem.at[0]
    )
    mine.start()
    my_bits = pltpu.make_async_copy(bits_ref, signs.at[me], local_sem.at[1])
    my_bits.start()

    barrier = pltpu.get_barrier_semaphore()

    def greet(s, carry):
        pl.semaphore_signal(
            barrier, inc=1, device_id={"cols": lax.rem(me + s, n)}, device_id_type=MESH
        )
        return carry

    lax.fori_loop(1, n, greet, 0)
    for r in range(1, n_rows):
        pl.semaphore_signal(
            barrier, inc=1, device_id={"rows": lax.rem(my_row + r, n_rows)}, device_id_type=MESH
        )
    table[...] = sylvester(local, scale)
    peaks[...] = jnp.zeros_like(peaks)
    pl.semaphore_wait(barrier, n - 1 + n_rows - 1)

    count = len(chunks)
    starts = [sum(chunks[:c]) for c in range(count)]

    def send_bits(s, carry):
        pltpu.make_async_remote_copy(
            src_ref=bits_ref, dst_ref=signs.at[me],
            send_sem=send_sem.at[count], recv_sem=recv_sem.at[count],
            device_id={"cols": peer_of(s)}, device_id_type=MESH,
        ).start()
        return carry

    lax.fori_loop(1, n, send_bits, 0)

    def send_chunk(c):
        def send(s, carry):
            p = peer_of(s)
            pltpu.make_async_remote_copy(
                src_ref=w_ref.at[pl.ds(pl.multiple_of(p * total + starts[c], 8), chunks[c])],
                dst_ref=recv.at[me, pl.ds(starts[c], chunks[c])],
                send_sem=send_sem.at[c], recv_sem=recv_sem.at[c],
                device_id={"cols": p}, device_id_type=MESH,
            ).start()
            return carry

        lax.fori_loop(1, n, send, 0)

    def wait_bytes(ref, sem):
        pltpu.make_async_copy(ref, ref, sem).wait()

    for c in range(min(2, count)):
        send_chunk(c)
    mine.wait()
    my_bits.wait()
    wait_bytes(signs.at[pl.ds(0, n - 1)], recv_sem.at[count])

    for c in range(count):
        if c + 2 < count:
            send_chunk(c + 2)
        r, r0, slot = chunks[c], starts[c], c % 2
        wait_bytes(recv.at[pl.ds(0, n - 1), pl.ds(r0, r)], recv_sem.at[c])

        def inner(a, carry):
            xs = []
            for b in range(8):
                d = a * 8 + b
                sign = (2 * signs[d] - 1).astype(jnp.float32)
                xs.append(recv[d, r0:r0 + r, :] * sign)
            for b, x in enumerate(butterfly(xs)):
                work[pl.ds(pl.multiple_of((a * 8 + b) * r, 8), r), :] = x
            return carry

        lax.fori_loop(0, n // 8, inner, 0)

        def outer(b, carry):
            at = [pl.ds(pl.multiple_of((a * 8 + b) * r, 8), r) for a in range(n // 8)]
            for where, z in zip(at, butterfly([work[where, :] for where in at])):
                work[where, :] = z
            return carry

        lax.fori_loop(0, 8, outer, 0)

        if c >= 2:
            wait_bytes(staged.at[slot, pl.ds(0, chunks[c - 2])], out_sem.at[slot])

        def product(m, carry):
            z = work[pl.ds(pl.multiple_of(m * TILE, TILE), TILE), :]
            high = z.astype(jnp.bfloat16)
            low = (z - high.astype(jnp.float32)).astype(jnp.bfloat16)
            y = jnp.dot(high, table[...], preferred_element_type=jnp.float32)
            y += jnp.dot(low, table[...], preferred_element_type=jnp.float32)
            for k in range(TILE // r):
                e = m * (TILE // r) + k
                block = y[k * r:(k + 1) * r, :]
                staged[slot, 0:r, pl.ds(pl.multiple_of(e * local, local), local)] = block.astype(jnp.bfloat16)
                size = jnp.abs(block)
                top = size[0:8]
                for q in range(1, r // 8):
                    top = jnp.maximum(top, size[8 * q:8 * q + 8])
                peaks[e] = jnp.maximum(peaks[e], top)
            return carry

        lax.fori_loop(0, n * r // TILE, product, 0)
        pltpu.make_async_copy(
            staged.at[slot, pl.ds(0, r)], out_ref.at[pl.ds(r0, r)], out_sem.at[slot]
        ).start()

    def shrink(e, carry):
        row_peaks[e] = jnp.max(peaks[e], axis=0, keepdims=True)
        return carry

    lax.fori_loop(0, n, shrink, 0)

    def send_peaks(s, carry):
        p = peer_of(s)
        pltpu.make_async_remote_copy(
            src_ref=row_peaks.at[p], dst_ref=col_in.at[me],
            send_sem=peak_sem.at[0], recv_sem=peak_sem.at[1],
            device_id={"cols": p}, device_id_type=MESH,
        ).start()
        return carry

    lax.fori_loop(1, n, send_peaks, 0)
    top = row_peaks[me]
    wait_bytes(col_in.at[pl.ds(0, n - 1)], peak_sem.at[1])
    col_in[me] = top
    top = jnp.max(col_in[...], axis=0)
    own[...] = top
    for r in range(1, n_rows):
        pltpu.make_async_remote_copy(
            src_ref=own, dst_ref=row_in.at[my_row],
            send_sem=peak_sem.at[2], recv_sem=peak_sem.at[3],
            device_id={"rows": lax.rem(my_row + r, n_rows)}, device_id_type=MESH,
        ).start()
    wait_bytes(row_in.at[pl.ds(0, n_rows - 1)], peak_sem.at[3])
    row_in[my_row] = top
    peak_ref[...] = jnp.max(row_in[...], axis=0)

    wait_bytes(row_peaks.at[pl.ds(0, n - 1)], peak_sem.at[0])
    wait_bytes(row_in.at[pl.ds(0, n_rows - 1)], peak_sem.at[2])
    wait_bytes(signs.at[pl.ds(0, n - 1)], send_sem.at[count])
    for c in range(count):
        wait_bytes(recv.at[pl.ds(0, n - 1), pl.ds(starts[c], chunks[c])], send_sem.at[c])
    for c in range(max(0, count - 2), count):
        wait_bytes(staged.at[c % 2, pl.ds(0, chunks[c])], out_sem.at[c % 2])


def body(weight, sign_bits):
    rows, local = weight.shape
    n, n_rows = lax.axis_size("cols"), lax.axis_size("rows")
    total, width = rows // n, local * n
    chunks = [BLOCK] * (total // BLOCK) + ([total % BLOCK] if total % BLOCK else [])
    out, peak = pl.pallas_call(
        functools.partial(kernel, n, n_rows, chunks, width ** -0.5),
        out_shape=(
            jax.ShapeDtypeStruct((total, width), jnp.bfloat16),
            jax.ShapeDtypeStruct((1, local), jnp.float32),
        ),
        in_specs=[pl.BlockSpec(memory_space=pl.ANY)] * 2,
        out_specs=(pl.BlockSpec(memory_space=pl.ANY), pl.BlockSpec(memory_space=pltpu.VMEM)),
        scratch_shapes=[
            pltpu.VMEM((n, total, local), jnp.float32),
            pltpu.VMEM((n, 1, local), jnp.int32),
            pltpu.VMEM((n * BLOCK, local), jnp.float32),
            pltpu.VMEM((local, local), jnp.bfloat16),
            pltpu.VMEM((2, BLOCK, width), jnp.bfloat16),
            pltpu.VMEM((n, 8, local), jnp.float32),
            pltpu.VMEM((n, 1, local), jnp.float32),
            pltpu.VMEM((n, 1, local), jnp.float32),
            pltpu.VMEM((1, local), jnp.float32),
            pltpu.VMEM((n_rows, 1, local), jnp.float32),
            pltpu.SemaphoreType.DMA((len(chunks) + 1,)),
            pltpu.SemaphoreType.DMA((len(chunks) + 1,)),
            pltpu.SemaphoreType.DMA((2,)),
            pltpu.SemaphoreType.DMA((2,)),
            pltpu.SemaphoreType.DMA((4,)),
        ],
        compiler_params=pltpu.CompilerParams(collective_id=0, has_side_effects=True),
        name="rotate",
    )(weight, sign_bits.reshape(1, local))
    return out, peak.reshape(local)


def solution(mesh):
    return jax.shard_map(
        body,
        mesh=mesh,
        in_specs=(P("rows", "cols"), P("cols")),
        out_specs=(P(("rows", "cols"), None), P("cols")),
        check_vma=False,
    )
```

```python
import functools

import jax
import jax.numpy as jnp
from jax import lax
from jax.experimental import pallas as pl
from jax.experimental.pallas import tpu as pltpu
from jax.sharding import PartitionSpec as P

MESH = pl.DeviceIdType.MESH
BLOCK = 16
TILE = 256
AHEAD = 2
SIDE = 4


def sylvester(order, scale):
    row = lax.broadcasted_iota(jnp.int32, (order, order), 0)
    column = lax.broadcasted_iota(jnp.int32, (order, order), 1)
    parity = row & column
    shift = order.bit_length() // 2
    while shift:
        parity = parity ^ (parity >> shift)
        shift //= 2
    return ((1 - 2 * (parity & 1)).astype(jnp.float32) * scale).astype(jnp.bfloat16)


def butterfly(values):
    values, step = list(values), 1
    while step < len(values):
        for start in range(0, len(values), 2 * step):
            for k in range(start, start + step):
                a, b = values[k], values[k + step]
                values[k], values[k + step] = a + b, a - b
        step *= 2
    return values


def kernel(
    n, n_rows, chunks, scale,
    w_ref, bits_ref, out_ref, peak_ref,
    recv, signs, work, table, peaks, row_peaks, peak_in, own, core_in,
    send_sem, recv_sem, local_sem, sign_send, sign_recv, peak_sem, hello,
):
    me = lax.axis_index("cols")
    my_row = lax.axis_index("rows")
    total, local = recv.shape[1], recv.shape[2]
    count = len(chunks)
    starts = [sum(chunks[:c]) for c in range(count)]
    y, z, x = me // 16, (me // 4) % 4, me % 4
    spot = y * 16 + x * 4 + z

    def at(yy, zz, xx):
        return yy * 16 + zz * 4 + xx

    def peer_of(s):
        zz, xx, yy = s & 3, (s >> 2) & 3, s >> 4
        return me ^ at(yy, zz, xx)

    def wait_bytes(ref, sem):
        pltpu.make_async_copy(ref, ref, sem).wait()

    mine = pltpu.make_async_copy(
        w_ref.at[pl.ds(pl.multiple_of(me * total, 8), total)], recv.at[me], local_sem.at[0]
    )
    mine.start()
    my_bits = pltpu.make_async_copy(bits_ref, signs.at[spot], local_sem.at[1])
    my_bits.start()

    barrier = pltpu.get_barrier_semaphore()
    for k in range(1, SIDE):
        for p in (me ^ at(0, k, 0), me ^ at(0, 0, k), me ^ at(k, 0, 0)):
            pl.semaphore_signal(barrier, inc=1, device_id={"cols": p}, device_id_type=MESH)
    mirror = {"rows": my_row ^ 2, "cols": me ^ at(0, SIDE - 1, 0)}
    pl.semaphore_signal(barrier, inc=1, device_id=mirror, device_id_type=MESH)
    core = my_row % 2
    twin = {"rows": my_row ^ 1}

    @pl.when(core == 0)
    def _():
        pl.semaphore_signal(barrier, inc=1, device_id=twin, device_id_type=MESH)

    table[...] = sylvester(local, scale)
    peaks[...] = jnp.zeros_like(peaks)
    my_bits.wait()
    pl.semaphore_wait(barrier, 3 * (SIDE - 1) + 1 + core)

    @pl.when(core == 1)
    def _():
        pl.semaphore_signal(hello, inc=1, device_id=twin, device_id_type=MESH)


    def send_signs(step, first, size, peers):
        for p in peers:
            pltpu.make_async_remote_copy(
                src_ref=signs.at[pl.ds(first, size)], dst_ref=signs.at[pl.ds(first, size)],
                send_sem=sign_send.at[step], recv_sem=sign_recv.at[step],
                device_id={"cols": p}, device_id_type=MESH,
            ).start()

    def wait_signs(step, size, sem):
        wait_bytes(signs.at[pl.ds(0, (SIDE - 1) * size)], sem.at[step])

    def send_rows(c, p):
        pltpu.make_async_remote_copy(
            src_ref=w_ref.at[pl.ds(pl.multiple_of(p * total + starts[c], 8), chunks[c])],
            dst_ref=recv.at[me, pl.ds(starts[c], chunks[c])],
            send_sem=send_sem.at[c], recv_sem=recv_sem.at[c],
            device_id={"cols": p}, device_id_type=MESH,
        ).start()

    def send_chunk(c):
        def send(s, carry):
            send_rows(c, peer_of(s))
            return carry

        lax.fori_loop(SIDE, n, send, 0)

    others = range(1, SIDE)
    send_signs(0, spot, 1, [me ^ at(0, k, 0) for k in others])
    for c in range(count):
        for k in others:
            send_rows(c, me ^ at(0, k, 0))
    wait_signs(0, 1, sign_recv)
    send_signs(1, y * 16 + x * 4, 4, [me ^ at(0, 0, k) for k in others])
    wait_signs(1, 4, sign_recv)
    send_signs(2, y * 16, 16, [me ^ at(k, 0, 0) for k in others])
    wait_signs(2, 16, sign_recv)

    for c in range(min(AHEAD, count)):
        send_chunk(c)
    mine.wait()

    for c in range(count):
        if c + AHEAD < count:
            send_chunk(c + AHEAD)
        r, r0 = chunks[c], starts[c]
        wait_bytes(recv.at[pl.ds(0, n - 1), pl.ds(r0, r)], recv_sem.at[c])

        def inner(a, carry):
            xs = []
            for b in range(8):
                d = a * 8 + b
                place = (d // 16) * 16 + (d % 4) * 4 + (d // 4) % 4
                sign = (2 * signs[place] - 1).astype(jnp.float32)
                xs.append(recv[d, r0:r0 + r, :] * sign)
            for b, v in enumerate(butterfly(xs)):
                work[pl.ds(pl.multiple_of((a * 8 + b) * r, 8), r), :] = v
            return carry

        lax.fori_loop(0, n // 8, inner, 0)

        def outer(b, carry):
            where = [pl.ds(pl.multiple_of((a * 8 + b) * r, 8), r) for a in range(n // 8)]
            for w, v in zip(where, butterfly([work[w, :] for w in where])):
                work[w, :] = v
            return carry

        lax.fori_loop(0, 8, outer, 0)

        def product(m, carry):
            v = work[pl.ds(pl.multiple_of(m * TILE, TILE), TILE), :]
            high = v.astype(jnp.bfloat16)
            low = (v - high.astype(jnp.float32)).astype(jnp.bfloat16)
            result = jnp.dot(high, table[...], preferred_element_type=jnp.float32)
            result += jnp.dot(low, table[...], preferred_element_type=jnp.float32)
            for k in range(TILE // r):
                e = m * (TILE // r) + k
                block = result[k * r:(k + 1) * r, :]
                out_ref[r0:r0 + r, pl.ds(pl.multiple_of(e * local, local), local)] = block.astype(jnp.bfloat16)
                size = jnp.abs(block)
                top = size[0:8]
                for q in range(1, r // 8):
                    top = jnp.maximum(top, size[8 * q:8 * q + 8])
                if c < count - 1:
                    peaks[e] = jnp.maximum(peaks[e], top)
                else:
                    row_peaks[e] = jnp.maximum(row_peaks[e], jnp.max(top, axis=0, keepdims=True))
            return carry

        lax.fori_loop(0, n * r // TILE, product, 0)
        if c == count - 2:

            def shrink(i, carry):
                for k in range(8):
                    row_peaks[i * 8 + k] = jnp.max(peaks[i * 8 + k], axis=0, keepdims=True)
                return carry

            lax.fori_loop(0, n // 8, shrink, 0)

    half = my_row // 2

    def send_peak(p, row):
        pltpu.make_async_remote_copy(
            src_ref=row_peaks.at[p], dst_ref=peak_in.at[half * n + me],
            send_sem=peak_sem.at[0], recv_sem=peak_sem.at[1],
            device_id={"cols": p, "rows": row}, device_id_type=MESH,
        ).start()

    for away, k in ((2, 0), (0, 3), (2, 1), (2, 3), (0, 2), (2, 2), (0, 1), (0, 0)):

        def to_plane(t, carry):
            send_peak(me ^ at((t // 4) ^ 2, k, (t % 4) ^ 2), my_row ^ away)
            return carry

        if (away, k) != (0, 0):
            lax.fori_loop(0, SIDE * SIDE, to_plane, 0)
        else:
            for t in range(SIDE * SIDE):
                if t != 10:
                    to_plane(t, 0)
    top = row_peaks[me]
    wait_bytes(peak_in.at[pl.ds(0, 2 * n - 1)], peak_sem.at[1])
    peak_in[half * n + me] = top
    top = jnp.max(peak_in[...], axis=0)
    own[...] = top

    @pl.when(core == 0)
    def _():
        pl.semaphore_wait(hello, 1)

    pltpu.make_async_remote_copy(
        src_ref=own, dst_ref=core_in, send_sem=peak_sem.at[2], recv_sem=peak_sem.at[3],
        device_id=twin, device_id_type=MESH,
    ).start()
    wait_bytes(core_in, peak_sem.at[3])
    peak_ref[...] = jnp.maximum(top, core_in[...])

    wait_bytes(own, peak_sem.at[2])
    wait_bytes(peak_in.at[pl.ds(0, 2 * n - 1)], peak_sem.at[0])
    for step, size in enumerate((1, 4, 16)):
        wait_signs(step, size, sign_send)
    for c in range(count):
        wait_bytes(recv.at[pl.ds(0, n - 1), pl.ds(starts[c], chunks[c])], send_sem.at[c])


def body(weight, sign_bits):
    rows, local = weight.shape
    n, n_rows = lax.axis_size("cols"), lax.axis_size("rows")
    total, width = rows // n, local * n
    chunks = [BLOCK] * (total // BLOCK) + ([total % BLOCK] if total % BLOCK else [])
    out, peak = pl.pallas_call(
        functools.partial(kernel, n, n_rows, chunks, width ** -0.5),
        out_shape=(
            pltpu.VMEM((total, width), jnp.bfloat16),
            pltpu.VMEM((1, local), jnp.float32),
        ),
        in_specs=[pl.BlockSpec(memory_space=pl.ANY)] * 2,
        out_specs=[pl.BlockSpec(memory_space=pltpu.VMEM)] * 2,
        scratch_shapes=[
            pltpu.VMEM((n, total, local), jnp.float32),
            pltpu.VMEM((n, 1, local), jnp.int32),
            pltpu.VMEM((n * BLOCK, local), jnp.float32),
            pltpu.VMEM((local, local), jnp.bfloat16),
            pltpu.VMEM((n, 8, local), jnp.float32),
            pltpu.VMEM((n, 1, local), jnp.float32),
            pltpu.VMEM((2 * n, 1, local), jnp.float32),
            pltpu.VMEM((1, local), jnp.float32),
            pltpu.VMEM((1, local), jnp.float32),
            pltpu.SemaphoreType.DMA((len(chunks),)),
            pltpu.SemaphoreType.DMA((len(chunks),)),
            pltpu.SemaphoreType.DMA((2,)),
            pltpu.SemaphoreType.DMA((3,)),
            pltpu.SemaphoreType.DMA((3,)),
            pltpu.SemaphoreType.DMA((4,)),
            pltpu.SemaphoreType.REGULAR,
        ],
        compiler_params=pltpu.CompilerParams(collective_id=0, has_side_effects=True, vmem_limit_bytes=58 << 20),
        name="rotate",
    )(weight, sign_bits.reshape(1, local))
    return out, peak.reshape(local)


def solution(mesh):
    return jax.shard_map(
        body,
        mesh=mesh,
        in_specs=(P("rows", "cols"), P("cols")),
        out_specs=(P(("rows", "cols"), None), P("cols")),
        check_vma=False,
    )
```

```python
import functools

import jax
import jax.numpy as jnp
from jax import lax
from jax.experimental import pallas as pl
from jax.experimental.pallas import tpu as pltpu
from jax.sharding import PartitionSpec as P

MESH = pl.DeviceIdType.MESH
BLOCK = 16
TILE = 256
PLANE = 3
AHEAD = 7
SIDE = 4


def sylvester(order, scale):
    row = lax.broadcasted_iota(jnp.int32, (order, order), 0)
    column = lax.broadcasted_iota(jnp.int32, (order, order), 1)
    parity = row & column
    shift = order.bit_length() // 2
    while shift:
        parity = parity ^ (parity >> shift)
        shift //= 2
    return ((1 - 2 * (parity & 1)).astype(jnp.float32) * scale).astype(jnp.bfloat16)


def butterfly(values):
    values, step = list(values), 1
    while step < len(values):
        for start in range(0, len(values), 2 * step):
            for k in range(start, start + step):
                a, b = values[k], values[k + step]
                values[k], values[k + step] = a + b, a - b
        step *= 2
    return values


def kernel(
    n, n_rows, chunks, scale,
    w_ref, bits_ref, out_ref, peak_ref,
    recv, signs, work, table, peaks, row_peaks, peak_in, own, core_in,
    send_sem, recv_sem, local_sem, sign_send, sign_recv, peak_sem, hello, word,
):
    me = lax.axis_index("cols")
    my_row = lax.axis_index("rows")
    total, local = recv.shape[1], recv.shape[2]
    count = len(chunks)
    starts = [sum(chunks[:c]) for c in range(count)]
    y, z, x = me // 16, (me // 4) % 4, me % 4
    spot = y * 16 + x * 4 + z

    def at(yy, zz, xx):
        return yy * 16 + zz * 4 + xx

    def peer_of(s):
        zz, xx, yy = s & 3, (s >> 2) & 3, s >> 4
        return me ^ at(yy, zz, xx)

    def wait_bytes(ref, sem):
        pltpu.make_async_copy(ref, ref, sem).wait()

    mine = pltpu.make_async_copy(
        w_ref.at[pl.ds(pl.multiple_of(me * total, 8), total)], recv.at[me], local_sem.at[0]
    )
    mine.start()
    my_bits = pltpu.make_async_copy(bits_ref, signs.at[spot], local_sem.at[1])
    my_bits.start()

    half, core = my_row // 2, my_row % 2
    twin = {"rows": my_row ^ 1}
    mirror = {"rows": my_row ^ 2, "cols": me ^ at(0, SIDE - 1, 0)}
    others = range(1, SIDE)

    def rank_z(v):
        return jnp.where(half == 0, v, 2 * jnp.minimum(v, SIDE - 1 - v) + v // 2)

    def rank(v):
        return v ^ (v // 2)

    line_z = [(me ^ at(0, k, 0), rank_z(z ^ k) < rank_z(z)) for k in others]
    line_x = [(me ^ at(0, 0, k), rank(x ^ k) < rank(x)) for k in others]
    line_y = [(me ^ at(k, 0, 0), rank(y ^ k) < rank(y)) for k in others]
    pairs = [({"cols": p}, earlier, 0) for p, earlier in line_z]
    pairs += [({"cols": p}, earlier, 1) for p, earlier in line_x + line_y]
    pairs += [(mirror, half == 1, 2), (twin, core == 1, 2)]

    def signal(sem, device):
        pl.semaphore_signal(sem, inc=1, device_id=device, device_id_type=MESH)

    def wait_some(sem, value):
        @pl.when(value > 0)
        def _():
            pl.semaphore_wait(sem, value)

    barrier = pltpu.get_barrier_semaphore()
    for device, earlier, _ in pairs:
        pl.when(jnp.logical_not(earlier))(functools.partial(signal, barrier, device))
    ahead_z, ahead_xy = rank_z(z), rank(x) + rank(y)
    wait_some(barrier, ahead_z + ahead_xy + half + core)
    for device, earlier, which in pairs:
        pl.when(earlier)(functools.partial(signal, hello.at[which], device))
    my_bits.wait()

    def send_signs(step, first, size, peers):
        for p in peers:
            pltpu.make_async_remote_copy(
                src_ref=signs.at[pl.ds(first, size)], dst_ref=signs.at[pl.ds(first, size)],
                send_sem=sign_send.at[step], recv_sem=sign_recv.at[step],
                device_id={"cols": p}, device_id_type=MESH,
            ).start()

    def wait_signs(step, size, sem):
        wait_bytes(signs.at[pl.ds(0, (SIDE - 1) * size)], sem.at[step])

    def send_rows(c, p):
        pltpu.make_async_remote_copy(
            src_ref=w_ref.at[pl.ds(pl.multiple_of(p * total + starts[c], 8), chunks[c])],
            dst_ref=recv.at[me, pl.ds(starts[c], chunks[c])],
            send_sem=send_sem.at[c], recv_sem=recv_sem.at[c],
            device_id={"cols": p}, device_id_type=MESH,
        ).start()

    def send_chunk(c, first, last):
        def send(s, carry):
            send_rows(c, peer_of(s))
            return carry

        lax.fori_loop(first, last, send, 0)

    plane = SIDE * SIDE

    def along_z(p):
        send_signs(0, spot, 1, [p])
        for c in range(count):
            send_rows(c, p)

    for p, earlier in line_z:
        pl.when(earlier)(functools.partial(along_z, p))
    table[...] = sylvester(local, scale)
    peaks[...] = jnp.zeros_like(peaks)
    wait_some(hello.at[0], SIDE - 1 - ahead_z)
    for p, earlier in line_z:
        pl.when(jnp.logical_not(earlier))(functools.partial(along_z, p))
    wait_some(hello.at[1], 2 * (SIDE - 1) - ahead_xy)
    wait_signs(0, 1, sign_recv)
    send_signs(1, y * 16 + x * 4, 4, [p for p, _ in line_x])
    wait_signs(1, 4, sign_recv)
    send_signs(2, y * 16, 16, [p for p, _ in line_y])
    for c in range(PLANE):
        send_chunk(c, SIDE, plane)
    wait_signs(2, 16, sign_recv)

    for c in range(min(AHEAD, count)):
        send_chunk(c, plane if c < PLANE else SIDE, n)
    mine.wait()

    for c in range(count):
        if c + AHEAD < count:
            send_chunk(c + AHEAD, plane if c + AHEAD < PLANE else SIDE, n)
        r, r0 = chunks[c], starts[c]
        wait_bytes(recv.at[pl.ds(0, n - 1), pl.ds(r0, r)], recv_sem.at[c])

        def inner(a, carry):
            xs = []
            for b in range(8):
                d = a * 8 + b
                place = (d // 16) * 16 + (d % 4) * 4 + (d // 4) % 4
                sign = (2 * signs[place] - 1).astype(jnp.float32)
                xs.append(recv[d, r0:r0 + r, :] * sign)
            for b, v in enumerate(butterfly(xs)):
                work[pl.ds(pl.multiple_of((a * 8 + b) * r, 8), r), :] = v
            return carry

        lax.fori_loop(0, n // 8, inner, 0)

        def outer(b, carry):
            where = [pl.ds(pl.multiple_of((a * 8 + b) * r, 8), r) for a in range(n // 8)]
            for w, v in zip(where, butterfly([work[w, :] for w in where])):
                work[w, :] = v
            return carry

        lax.fori_loop(0, 8, outer, 0)

        def product(m, carry):
            v = work[pl.ds(pl.multiple_of(m * TILE, TILE), TILE), :]
            high = v.astype(jnp.bfloat16)
            low = (v - high.astype(jnp.float32)).astype(jnp.bfloat16)
            result = jnp.dot(high, table[...], preferred_element_type=jnp.float32)
            result += jnp.dot(low, table[...], preferred_element_type=jnp.float32)
            for k in range(TILE // r):
                e = m * (TILE // r) + k
                block = result[k * r:(k + 1) * r, :]
                out_ref[r0:r0 + r, pl.ds(pl.multiple_of(e * local, local), local)] = block.astype(jnp.bfloat16)
                size = jnp.abs(block)
                top = size[0:8]
                for q in range(1, r // 8):
                    top = jnp.maximum(top, size[8 * q:8 * q + 8])
                if c < count - 1:
                    peaks[e] = jnp.maximum(peaks[e], top)
                else:
                    row_peaks[e] = jnp.maximum(row_peaks[e], jnp.max(top, axis=0, keepdims=True))
            return carry

        lax.fori_loop(0, n * r // TILE, product, 0)
        if c == 1:
            wait_some(hello.at[2], 2 - half - core)
            for step, devices in enumerate((
                [mirror, twin], *([{"cols": p} for p, _ in line] for line in (line_z, line_x, line_y)),
            )):
                for device in devices:
                    signal(word.at[step], device)
                pl.semaphore_wait(word.at[step], len(devices))
        if c == count - 2:

            def shrink(i, carry):
                for k in range(8):
                    row_peaks[i * 8 + k] = jnp.max(peaks[i * 8 + k], axis=0, keepdims=True)
                return carry

            lax.fori_loop(0, n // 8, shrink, 0)


    def send_peak(p, row):
        pltpu.make_async_remote_copy(
            src_ref=row_peaks.at[p], dst_ref=peak_in.at[my_row * n + me],
            send_sem=peak_sem.at[0], recv_sem=peak_sem.at[1],
            device_id={"cols": p, "rows": row}, device_id_type=MESH,
        ).start()

    for away, k in ((2, 0), (0, 3), (2, 1), (2, 3), (0, 2), (2, 2), (0, 1), (0, 0)):

        def to_plane(t, carry):
            send_peak(me ^ at((t // 4) ^ 2, k, (t % 4) ^ 2), (half * 2) ^ away)
            return carry

        if (away, k) != (0, 0):
            lax.fori_loop(0, SIDE * SIDE, to_plane, 0)
        else:
            for t in range(SIDE * SIDE):
                if t != 10:
                    to_plane(t, 0)

    @pl.when(core == 1)
    def _():
        send_peak(me, my_row ^ 1)
        wait_bytes(core_in, peak_sem.at[3])
        peak_ref[...] = core_in[...]
        wait_bytes(row_peaks, peak_sem.at[0])
        wait_bytes(row_peaks, peak_sem.at[0])

    @pl.when(core == 0)
    def _():
        top = row_peaks[me]
        wait_bytes(peak_in.at[pl.ds(0, n_rows * n - 1)], peak_sem.at[1])
        peak_in[my_row * n + me] = top
        top = jnp.max(peak_in[...], axis=0)
        own[...] = top
        last = pltpu.make_async_remote_copy(
            src_ref=own, dst_ref=core_in, send_sem=peak_sem.at[2], recv_sem=peak_sem.at[3],
            device_id=twin, device_id_type=MESH,
        )
        last.start()
        peak_ref[...] = top
        wait_bytes(peak_in.at[pl.ds(0, 2 * n - 1)], peak_sem.at[0])
        last.wait_send()

    for step, size in enumerate((1, 4, 16)):
        wait_signs(step, size, sign_send)
    for c in range(count):
        wait_bytes(recv.at[pl.ds(0, n - 1), pl.ds(starts[c], chunks[c])], send_sem.at[c])


def store(out_ref, peak_ref, out_hbm, peak_hbm, sem):
    rows = out_ref.shape[0]
    copies = [(peak_ref, peak_hbm)]
    copies += [(out_ref.at[pl.ds(i, 8)], out_hbm.at[pl.ds(i, 8)]) for i in range(0, rows, 8)]
    copies = [pltpu.make_async_copy(a, b, sem.at[i]) for i, (a, b) in enumerate(copies)]
    for copy in copies:
        copy.start()
    for copy in copies:
        copy.wait()


def body(weight, sign_bits):
    rows, local = weight.shape
    n, n_rows = lax.axis_size("cols"), lax.axis_size("rows")
    total, width = rows // n, local * n
    chunks = [BLOCK] * (total // BLOCK) + ([total % BLOCK] if total % BLOCK else [])
    out, peak = pl.pallas_call(
        functools.partial(kernel, n, n_rows, chunks, width ** -0.5),
        out_shape=(
            pltpu.VMEM((total, width), jnp.bfloat16),
            pltpu.VMEM((1, local), jnp.float32),
        ),
        in_specs=[pl.BlockSpec(memory_space=pl.ANY)] * 2,
        out_specs=[pl.BlockSpec(memory_space=pltpu.VMEM)] * 2,
        scratch_shapes=[
            pltpu.VMEM((n, total, local), jnp.float32),
            pltpu.VMEM((n, 1, local), jnp.int32),
            pltpu.VMEM((n * BLOCK, local), jnp.float32),
            pltpu.VMEM((local, local), jnp.bfloat16),
            pltpu.VMEM((n, 8, local), jnp.float32),
            pltpu.VMEM((n, 1, local), jnp.float32),
            pltpu.VMEM((n_rows * n, 1, local), jnp.float32),
            pltpu.VMEM((1, local), jnp.float32),
            pltpu.VMEM((1, local), jnp.float32),
            pltpu.SemaphoreType.DMA((len(chunks),)),
            pltpu.SemaphoreType.DMA((len(chunks),)),
            pltpu.SemaphoreType.DMA((2,)),
            pltpu.SemaphoreType.DMA((3,)),
            pltpu.SemaphoreType.DMA((3,)),
            pltpu.SemaphoreType.DMA((4,)),
            pltpu.SemaphoreType.REGULAR((3,)),
            pltpu.SemaphoreType.REGULAR((4,)),
        ],
        compiler_params=pltpu.CompilerParams(collective_id=0, has_side_effects=True, vmem_limit_bytes=58 << 20),
        name="rotate",
    )(weight, sign_bits.reshape(1, local))
    out, peak = pl.pallas_call(
        store,
        out_shape=(
            jax.ShapeDtypeStruct((total, width), jnp.bfloat16),
            jax.ShapeDtypeStruct((1, local), jnp.float32),
        ),
        in_specs=[pl.BlockSpec(memory_space=pl.ANY)] * 2,
        out_specs=[pl.BlockSpec(memory_space=pl.ANY)] * 2,
        scratch_shapes=[pltpu.SemaphoreType.DMA((total // 8 + 1,))],
        compiler_params=pltpu.CompilerParams(vmem_limit_bytes=1 << 20),
        name="store",
    )(out, peak)
    return out, peak.reshape(local)


def solution(mesh):
    return jax.shard_map(
        body,
        mesh=mesh,
        in_specs=(P("rows", "cols"), P("cols")),
        out_specs=(P(("rows", "cols"), None), P("cols")),
        check_vma=False,
    )
```

```python
import functools

import jax
import jax.numpy as jnp
from jax import lax
from jax.experimental import pallas as pl
from jax.experimental.pallas import tpu as pltpu
from jax.sharding import PartitionSpec as P

MESH = pl.DeviceIdType.MESH
BLOCK = 16
TILE = 256
PLANE = 3
AHEAD = 7
SIDE = 4


def sylvester(order, scale):
    row = lax.broadcasted_iota(jnp.int32, (order, order), 0)
    column = lax.broadcasted_iota(jnp.int32, (order, order), 1)
    parity = row & column
    shift = order.bit_length() // 2
    while shift:
        parity = parity ^ (parity >> shift)
        shift //= 2
    return ((1 - 2 * (parity & 1)).astype(jnp.float32) * scale).astype(jnp.bfloat16)


def butterfly(values):
    values, step = list(values), 1
    while step < len(values):
        for start in range(0, len(values), 2 * step):
            for k in range(start, start + step):
                a, b = values[k], values[k + step]
                values[k], values[k + step] = a + b, a - b
        step *= 2
    return values


def kernel(
    n, n_rows, chunks, scale,
    w_ref, bits_ref, out_ref, peak_ref,
    recv, signs, work, table, peaks, row_peaks, peak_in, own, core_in,
    send_sem, recv_sem, local_sem, sign_send, sign_recv, peak_sem, hello, word,
):
    me = lax.axis_index("cols")
    my_row = lax.axis_index("rows")
    total, local = recv.shape[1], recv.shape[2]
    count = len(chunks)
    starts = [sum(chunks[:c]) for c in range(count)]
    y, z, x = me // 16, (me // 4) % 4, me % 4
    spot = y * 16 + x * 4 + z

    def at(yy, zz, xx):
        return yy * 16 + zz * 4 + xx

    def peer_of(s):
        zz, xx, yy = s & 3, (s >> 2) & 3, s >> 4
        return me ^ at(yy, zz, xx)

    def wait_bytes(ref, sem):
        pltpu.make_async_copy(ref, ref, sem).wait()

    mine = pltpu.make_async_copy(
        w_ref.at[pl.ds(pl.multiple_of(me * total, 8), total)], recv.at[me], local_sem.at[0]
    )
    mine.start()
    my_bits = pltpu.make_async_copy(bits_ref, signs.at[spot], local_sem.at[1])
    my_bits.start()

    half, core = my_row // 2, my_row % 2
    twin = {"rows": my_row ^ 1}
    mirror = {"rows": my_row ^ 2, "cols": me ^ at(0, SIDE - 1, 0)}
    others = range(1, SIDE)

    def rank_z(v):
        return jnp.where(half == 0, v, 2 * jnp.minimum(v, SIDE - 1 - v) + v // 2)

    def rank(v):
        return v ^ (v // 2)

    line_z = [(me ^ at(0, k, 0), rank_z(z ^ k) < rank_z(z)) for k in others]
    line_x = [(me ^ at(0, 0, k), rank(x ^ k) < rank(x)) for k in others]
    line_y = [(me ^ at(k, 0, 0), rank(y ^ k) < rank(y)) for k in others]
    pairs = [({"cols": p}, earlier, 0) for p, earlier in line_z]
    pairs += [({"cols": p}, earlier, 1) for p, earlier in line_x + line_y]
    pairs += [(mirror, half == 1, 2), (twin, core == 1, 2)]

    def signal(sem, device):
        pl.semaphore_signal(sem, inc=1, device_id=device, device_id_type=MESH)

    def wait_some(sem, value):
        @pl.when(value > 0)
        def _():
            pl.semaphore_wait(sem, value)

    barrier = pltpu.get_barrier_semaphore()
    for device, earlier, _ in pairs:
        pl.when(jnp.logical_not(earlier))(functools.partial(signal, barrier, device))
    ahead_z, ahead_xy = rank_z(z), rank(x) + rank(y)
    wait_some(barrier, ahead_z + ahead_xy + half + core)
    for device, earlier, which in pairs:
        pl.when(earlier)(functools.partial(signal, hello.at[which], device))
    my_bits.wait()

    def send_signs(step, first, size, peers):
        for p in peers:
            pltpu.make_async_remote_copy(
                src_ref=signs.at[pl.ds(first, size)], dst_ref=signs.at[pl.ds(first, size)],
                send_sem=sign_send.at[step], recv_sem=sign_recv.at[step],
                device_id={"cols": p}, device_id_type=MESH,
            ).start()

    def wait_signs(step, size, sem):
        wait_bytes(signs.at[pl.ds(0, (SIDE - 1) * size)], sem.at[step])

    def send_rows(c, p):
        pltpu.make_async_remote_copy(
            src_ref=w_ref.at[pl.ds(pl.multiple_of(p * total + starts[c], 8), chunks[c])],
            dst_ref=recv.at[me, pl.ds(starts[c], chunks[c])],
            send_sem=send_sem.at[c], recv_sem=recv_sem.at[c],
            device_id={"cols": p}, device_id_type=MESH,
        ).start()

    def send_chunk(c, first, last):
        def send(s, carry):
            send_rows(c, peer_of(s))
            return carry

        lax.fori_loop(first, last, send, 0)

    plane = SIDE * SIDE

    def along_z(p):
        send_signs(0, spot, 1, [p])
        for c in range(count):
            send_rows(c, p)

    for p, earlier in line_z:
        pl.when(earlier)(functools.partial(along_z, p))
    table[...] = sylvester(local, scale)
    peaks[...] = jnp.zeros_like(peaks)
    wait_some(hello.at[0], SIDE - 1 - ahead_z)
    for p, earlier in line_z:
        pl.when(jnp.logical_not(earlier))(functools.partial(along_z, p))
    wait_some(hello.at[1], 2 * (SIDE - 1) - ahead_xy)
    wait_signs(0, 1, sign_recv)
    send_signs(1, y * 16 + x * 4, 4, [p for p, _ in line_x])
    wait_signs(1, 4, sign_recv)
    send_signs(2, y * 16, 16, [p for p, _ in line_y])
    for c in range(PLANE):
        send_chunk(c, SIDE, plane)
    wait_signs(2, 16, sign_recv)

    for c in range(min(AHEAD, count)):
        send_chunk(c, plane if c < PLANE else SIDE, n)
    mine.wait()

    for c in range(count):
        if c + AHEAD < count:
            send_chunk(c + AHEAD, plane if c + AHEAD < PLANE else SIDE, n)
        r, r0 = chunks[c], starts[c]
        tile = 512 if c == count - 1 else TILE
        wait_bytes(recv.at[pl.ds(0, n - 1), pl.ds(r0, r)], recv_sem.at[c])

        def inner(a, carry):
            xs = []
            for b in range(8):
                d = a * 8 + b
                place = (d // 16) * 16 + (d % 4) * 4 + (d // 4) % 4
                sign = (2 * signs[place] - 1).astype(jnp.float32)
                xs.append(recv[d, r0:r0 + r, :] * sign)
            for b, v in enumerate(butterfly(xs)):
                work[pl.ds(pl.multiple_of((a * 8 + b) * r, 8), r), :] = v
            return carry

        lax.fori_loop(0, n // 8, inner, 0)

        def outer(b, carry):
            where = [pl.ds(pl.multiple_of((a * 8 + b) * r, 8), r) for a in range(n // 8)]
            for w, v in zip(where, butterfly([work[w, :] for w in where])):
                work[w, :] = v
            return carry

        lax.fori_loop(0, 8, outer, 0)

        def product(m, carry):
            v = work[pl.ds(pl.multiple_of(m * tile, tile), tile), :]
            high = v.astype(jnp.bfloat16)
            low = (v - high.astype(jnp.float32)).astype(jnp.bfloat16)
            result = jnp.dot(high, table[...], preferred_element_type=jnp.float32)
            result += jnp.dot(low, table[...], preferred_element_type=jnp.float32)
            for k in range(tile // r):
                e = m * (tile // r) + k
                block = result[k * r:(k + 1) * r, :]
                out_ref[r0:r0 + r, pl.ds(pl.multiple_of(e * local, local), local)] = block.astype(jnp.bfloat16)
                size = jnp.abs(block)
                top = size[0:8]
                for q in range(1, r // 8):
                    top = jnp.maximum(top, size[8 * q:8 * q + 8])
                if c < count - 1:
                    peaks[e] = jnp.maximum(peaks[e], top)
                else:
                    row_peaks[e] = jnp.maximum(row_peaks[e], jnp.max(top, axis=0, keepdims=True))
            return carry

        lax.fori_loop(0, n * r // tile, product, 0)
        if c == 1:
            wait_some(hello.at[2], 2 - half - core)
            for step, devices in enumerate((
                [mirror, twin], *([{"cols": p} for p, _ in line] for line in (line_z, line_x, line_y)),
            )):
                for device in devices:
                    signal(word.at[step], device)
                pl.semaphore_wait(word.at[step], len(devices))
        if c == count - 2:

            def shrink(i, carry):
                for k in range(8):
                    row_peaks[i * 8 + k] = jnp.max(peaks[i * 8 + k], axis=0, keepdims=True)
                return carry

            lax.fori_loop(0, n // 8, shrink, 0)


    def send_peak(p, row):
        pltpu.make_async_remote_copy(
            src_ref=row_peaks.at[p], dst_ref=peak_in.at[my_row * n + me],
            send_sem=peak_sem.at[0], recv_sem=peak_sem.at[1],
            device_id={"cols": p, "rows": row}, device_id_type=MESH,
        ).start()

    for away, k in ((2, 0), (2, 1), (2, 3), (2, 2), (0, 3), (0, 2), (0, 1), (0, 0)):

        def to_plane(t, carry):
            send_peak(me ^ at((t // 4) ^ 2, k, (t % 4) ^ 2), (half * 2) ^ away)
            return carry

        if (away, k) != (0, 0):
            lax.fori_loop(0, SIDE * SIDE, to_plane, 0)
        else:
            for t in range(SIDE * SIDE):
                if t != 10:
                    to_plane(t, 0)

    @pl.when(core == 1)
    def _():
        send_peak(me, my_row ^ 1)
        wait_bytes(core_in, peak_sem.at[3])
        peak_ref[...] = core_in[...]
        wait_bytes(row_peaks, peak_sem.at[0])
        wait_bytes(row_peaks, peak_sem.at[0])

    @pl.when(core == 0)
    def _():
        top = row_peaks[me]
        wait_bytes(peak_in.at[pl.ds(0, n_rows * n - 1)], peak_sem.at[1])
        peak_in[my_row * n + me] = top
        top = jnp.max(peak_in[...], axis=0)
        own[...] = top
        last = pltpu.make_async_remote_copy(
            src_ref=own, dst_ref=core_in, send_sem=peak_sem.at[2], recv_sem=peak_sem.at[3],
            device_id=twin, device_id_type=MESH,
        )
        last.start()
        peak_ref[...] = top
        wait_bytes(peak_in.at[pl.ds(0, 2 * n - 1)], peak_sem.at[0])
        last.wait_send()

    for step, size in enumerate((1, 4, 16)):
        wait_signs(step, size, sign_send)
    for c in range(count):
        wait_bytes(recv.at[pl.ds(0, n - 1), pl.ds(starts[c], chunks[c])], send_sem.at[c])


def store(out_ref, peak_ref, out_hbm, peak_hbm, sem):
    rows = out_ref.shape[0]
    copies = [(peak_ref, peak_hbm)]
    copies += [(out_ref.at[pl.ds(i, 8)], out_hbm.at[pl.ds(i, 8)]) for i in range(0, rows, 8)]
    copies = [pltpu.make_async_copy(a, b, sem.at[i]) for i, (a, b) in enumerate(copies)]
    for copy in copies:
        copy.start()
    for copy in copies:
        copy.wait()


def body(weight, sign_bits):
    rows, local = weight.shape
    n, n_rows = lax.axis_size("cols"), lax.axis_size("rows")
    total, width = rows // n, local * n
    chunks = [BLOCK] * (total // BLOCK) + ([total % BLOCK] if total % BLOCK else [])
    out, peak = pl.pallas_call(
        functools.partial(kernel, n, n_rows, chunks, width ** -0.5),
        out_shape=(
            pltpu.VMEM((total, width), jnp.bfloat16),
            pltpu.VMEM((1, local), jnp.float32),
        ),
        in_specs=[pl.BlockSpec(memory_space=pl.ANY)] * 2,
        out_specs=[pl.BlockSpec(memory_space=pltpu.VMEM)] * 2,
        scratch_shapes=[
            pltpu.VMEM((n, total, local), jnp.float32),
            pltpu.VMEM((n, 1, local), jnp.int32),
            pltpu.VMEM((n * BLOCK, local), jnp.float32),
            pltpu.VMEM((local, local), jnp.bfloat16),
            pltpu.VMEM((n, 8, local), jnp.float32),
            pltpu.VMEM((n, 1, local), jnp.float32),
            pltpu.VMEM((n_rows * n, 1, local), jnp.float32),
            pltpu.VMEM((1, local), jnp.float32),
            pltpu.VMEM((1, local), jnp.float32),
            pltpu.SemaphoreType.DMA((len(chunks),)),
            pltpu.SemaphoreType.DMA((len(chunks),)),
            pltpu.SemaphoreType.DMA((2,)),
            pltpu.SemaphoreType.DMA((3,)),
            pltpu.SemaphoreType.DMA((3,)),
            pltpu.SemaphoreType.DMA((4,)),
            pltpu.SemaphoreType.REGULAR((3,)),
            pltpu.SemaphoreType.REGULAR((4,)),
        ],
        compiler_params=pltpu.CompilerParams(collective_id=0, has_side_effects=True, vmem_limit_bytes=58 << 20),
        name="rotate",
    )(weight, sign_bits.reshape(1, local))
    out, peak = pl.pallas_call(
        store,
        out_shape=(
            jax.ShapeDtypeStruct((total, width), jnp.bfloat16),
            jax.ShapeDtypeStruct((1, local), jnp.float32),
        ),
        in_specs=[pl.BlockSpec(memory_space=pl.ANY)] * 2,
        out_specs=[pl.BlockSpec(memory_space=pl.ANY)] * 2,
        scratch_shapes=[pltpu.SemaphoreType.DMA((total // 8 + 1,))],
        compiler_params=pltpu.CompilerParams(vmem_limit_bytes=1 << 20),
        name="store",
    )(out, peak)
    return out, peak.reshape(local)


def solution(mesh):
    return jax.shard_map(
        body,
        mesh=mesh,
        in_specs=(P("rows", "cols"), P("cols")),
        out_specs=(P(("rows", "cols"), None), P("cols")),
        check_vma=False,
    )
```
